32 devices in a mesh: segment: 2 (over x), lat: 4 (over y, core), lon: 4 (over z).
Axes of the slice: x: 2, y: 2, z: 4, core: 2. Of those that a mesh axis runs over, the one named last changes fastest.
Arguments:
- segment_input: bfloat16 [2, 32, 256, 128], P('segment', 'lat', 'lon'), may hold values from -6 to 6
- weights: bfloat16 [2, 2, 3, 3, 128, 128], P('segment'), may hold values from -0.1875 to 0.1875
- biases: float32 [2, 2, 128], P('segment'), may hold values from -3 to 3
- out_grad: bfloat16 [2, 32, 256, 128], P('segment', 'lat', 'lon'), may hold values from -6 to 6
Outputs:
- weight_grad: float32 [2, 2, 3, 3, 128, 128], P('segment')
- bias_grad: float32 [2, 2, 128], P('segment')
- input_grad: bfloat16 [2, 32, 256, 128], P('segment', 'lat', 'lon')
- skip_grad: bfloat16 [2, 16, 128, 128], P('segment', 'lat', 'lon')
The draws below stay inside these ranges and needn't reach their ends.
All inputs are finite; a program needn't handle non-finite values.
Results may differ from the reference program's by a relative error of at most 0.006.
Values may be sent and summed in bfloat16 or wider, within the bound.
A program may use at most 64 MiB of HBM per device.

```python
import math
import jax
import jax.numpy as jnp
from jax import lax

C = 128
NLAT = 32
NLON = 256
N_SEGMENT = 2


def block_levels(own_key, extent, pieces, smallest, largest):
    gain, own = 1.0, jax.random.fold_in(own_key, 6)
    for axis_at, blocks in pieces:
        heights = jnp.exp(jax.random.uniform(jax.random.fold_in(own, axis_at), (blocks,), jnp.float32, smallest / len(pieces), largest / len(pieces)))
        gain = gain * jnp.repeat(heights, extent[axis_at] // blocks).reshape([-1 if axis == axis_at else 1 for axis in range(len(extent))])
    return gain


def noise(key, shape, spread, limit, cuts=(), held_as=jnp.bfloat16):
    drawn = spread * jax.random.normal(key, shape, jnp.float32)
    if cuts:
        drawn = drawn * block_levels(key, shape, cuts, -0.22, 0.18)
    return jnp.clip(drawn, -limit, limit).astype(held_as)


def setup_inputs(seed: int = 0) -> dict:
    key_of = jax.random.split(jax.random.key(seed), 5)
    return {
        "segment_input": noise(key_of[0], (N_SEGMENT, NLAT, NLON, C), 1.0, 6.0, ((0, 2), (1, 4), (2, 4))),
        "weights": noise(key_of[1], (N_SEGMENT, 2, 3, 3, C, C), (9 * C) ** -0.5, 0.1875, ((0, 2),)),
        "biases": noise(key_of[2], (N_SEGMENT, 2, C), 0.5, 3.0, ((0, 2),), jnp.float32),
        "out_grad": noise(key_of[3], (N_SEGMENT, NLAT, NLON, C), 1.0, 6.0, ((0, 2), (1, 4), (2, 4))),
    }


def wrap_pad(field):
    tall = jnp.pad(field, ((1, 1), (0, 0), (0, 0)))
    return jnp.concatenate([tall[:, -1:], tall, tall[:, :1]], axis=1)

def convolve(padded, kernel):
    height = padded.shape[0] - 2
    width = padded.shape[1] - 2
    total = jnp.zeros((height, width, kernel.shape[3]), jnp.float32)
    for p in range(3):
        for q in range(3):
            total = total + jnp.dot(padded[p:p + height, q:q + width], kernel[p, q], preferred_element_type=jnp.float32)
    return total

def transpose_conv(padded, kernel):
    height = padded.shape[0] - 2
    width = padded.shape[1] - 2
    total = jnp.zeros((height, width, kernel.shape[2]), jnp.float32)
    for p in range(3):
        for q in range(3):
            total = total + jnp.dot(padded[2 - p:2 - p + height, 2 - q:2 - q + width], kernel[p, q].T, preferred_element_type=jnp.float32)
    return total

def correlate(padded, grad):
    height, width, chans = grad.shape
    flat_grad = grad.reshape(height * width, chans)
    rows_out = []
    for p in range(3):
        cols_out = []
        for q in range(3):
            piece = padded[p:p + height, q:q + width].reshape(height * width, -1)
            cols_out.append(jnp.dot(piece.T, flat_grad, preferred_element_type=jnp.float32))
        rows_out.append(jnp.stack(cols_out))
    return jnp.stack(rows_out)

def slope(value):
    sig = jax.nn.sigmoid(value)
    return sig * (1.0 + value * (1.0 - sig))

def section(source, kernel, shift_b, upstream):
    padded_in = wrap_pad(source)
    pre_first = convolve(padded_in, kernel[0]) + shift_b[0]
    act_pad = wrap_pad(jax.nn.silu(pre_first).astype(jnp.bfloat16))
    pre_second = convolve(act_pad, kernel[1]) + shift_b[1]
    grad_second = (upstream.astype(jnp.float32) * slope(pre_second)).astype(jnp.bfloat16)
    w_second = correlate(act_pad, grad_second)
    b_second = lax.optimization_barrier(jnp.sum(grad_second.astype(jnp.float32), axis=(0, 1)))
    grad_act = transpose_conv(wrap_pad(grad_second), kernel[1])
    grad_first = (grad_act * slope(pre_first)).astype(jnp.bfloat16)
    w_first = correlate(padded_in, grad_first)
    b_first = lax.optimization_barrier(jnp.sum(grad_first.astype(jnp.float32), axis=(0, 1)))
    grad_in = transpose_conv(wrap_pad(grad_first), kernel[0])
    scale = 1.0 / math.sqrt(NLAT * NLON)
    pooled = grad_in.reshape(NLAT // 2, 2, NLON // 2, 2, -1).sum(axis=(1, 3)).astype(jnp.bfloat16)
    return (jnp.stack([w_first, w_second]) * scale, jnp.stack([b_first, b_second]) * scale, grad_in.astype(jnp.bfloat16), pooled)

def reference(segment_input, weights, biases, out_grad):
    results = [section(segment_input[s], weights[s], biases[s], out_grad[s]) for s in range(N_SEGMENT)]
    weight_grad = jnp.stack([r[0] for r in results])
    bias_grad = jnp.stack([r[1] for r in results])
    input_grad = jnp.stack([r[2] for r in results])
    skip_grad = jnp.stack([results[1][3], jnp.zeros_like(results[1][3])])
    return (weight_grad, bias_grad, input_grad, skip_grad)
```

```python
import functools
import math

import jax
import jax.numpy as jnp
from jax import lax
from jax.experimental import pallas as pl
from jax.experimental.pallas import tpu as pltpu
from jax.sharding import PartitionSpec as P

MESH = pl.DeviceIdType.MESH
F32 = jnp.float32
BF16 = jnp.bfloat16
PAD = 8
XROWS = 4
GROWS = 2
RELATIONS = ((1, 0), (-1, 0), (0, 1), (0, -1), (1, 1), (1, -1), (-1, 1), (-1, -1))


def triple(field, forward):
    count = field.shape[0]
    before = pltpu.roll(field, 1, 0).astype(BF16)
    after = pltpu.roll(field, count - 1, 0).astype(BF16)
    if forward:
        return before, field.astype(BF16), after
    return after, field.astype(BF16), before


def slope(value, sig):
    return sig * (1.0 + value * (1.0 - sig))


def kernel(sizes, x_hbm, w_hbm, b_hbm, g_hbm,
           wout, bout, gin, skip,
           xin, gin_buf, b_ref, wv, wt,
           xn, xs, xw, xe, xnw, xne, xsw, xse,
           gn, gs, gw, ge, gnw, gne, gsw, gse,
           x3, a3, g3, p3, s1,
           part, rc, m1, rl, mid, rn, bpart, bmid,
           pool32, pool, skip_in,
           local_sem, halo_send, halo_recv, red_send, red_recv, skip_send, skip_recv):
    nseg, L, N, H, W, C, S, used, scale = sizes
    WP, L2 = W + 2 * PAD, L // 2
    seg, lat, lon = lax.axis_index("segment"), lax.axis_index("lat"), lax.axis_index("lon")

    loads = [
        pltpu.make_async_copy(w_hbm, wv, local_sem.at[0]),
        pltpu.make_async_copy(x_hbm, xin, local_sem.at[1]),
        pltpu.make_async_copy(g_hbm, gin_buf, local_sem.at[2]),
        pltpu.make_async_copy(b_hbm, b_ref, local_sem.at[3]),
    ]
    for load in loads:
        load.start()

    def lat_peer(d):
        return lax.rem(lat + d, L)

    def lon_peer(d):
        return lax.rem(lon + (d + N), N)

    barrier = pltpu.get_barrier_semaphore()

    def greet(s, a, o):
        pl.semaphore_signal(barrier, inc=1, device_id=(s, a, o), device_id_type=MESH)

    for d in range(1, L):
        greet(seg, lat_peer(d), lon)
    for d in range(1, N):
        greet(seg, lat, lon_peer(d))

    @pl.when(lat > 0)
    def _():
        greet(seg, lat - 1, lon_peer(1))
        greet(seg, lat - 1, lon_peer(-1))

    @pl.when(lat < L - 1)
    def _():
        greet(seg, lat + 1, lon_peer(1))
        greet(seg, lat + 1, lon_peer(-1))

    @pl.when(seg > 0)
    def _():
        greet(seg - 1, lat, lon)

    @pl.when(seg < nseg - 1)
    def _():
        greet(seg + 1, lat, lon)

    def flag(condition):
        return lax.convert_element_type(condition, jnp.int32)

    peers = (L - 1 + N - 1 + 2 * flag(lat > 0) + 2 * flag(lat < L - 1)
             + flag(seg > 0) + flag(seg < nseg - 1))
    pl.semaphore_wait(barrier, peers)

    xdst = {(1, 0): xn, (-1, 0): xs, (0, 1): xw, (0, -1): xe,
            (1, 1): xnw, (1, -1): xne, (-1, 1): xsw, (-1, -1): xse}
    gdst = {(1, 0): gn, (-1, 0): gs, (0, 1): gw, (0, -1): ge,
            (1, 1): gnw, (1, -1): gne, (-1, 1): gsw, (-1, -1): gse}

    def piece(ref, rows, dl, do):
        r = {1: pl.ds(H - rows, rows), -1: pl.ds(0, rows), 0: pl.ds(0, H)}[dl]
        c = {1: pl.ds(W - PAD, PAD), -1: pl.ds(0, PAD), 0: pl.ds(0, W)}[do]
        return ref.at[r, c]

    def halo_copy(which, k):
        dl, do = RELATIONS[k]
        ref, rows, dst = (x_hbm, XROWS, xdst) if which == 0 else (g_hbm, GROWS, gdst)
        at = which * len(RELATIONS) + k
        return pltpu.make_async_remote_copy(
            src_ref=piece(ref, rows, dl, do),
            dst_ref=dst[(dl, do)],
            send_sem=halo_send.at[at],
            recv_sem=halo_recv.at[at],
            device_id=(seg, lat + dl, lon_peer(do)),
            device_id_type=MESH,
        )

    def halo_each(which, act):
        for k, (dl, do) in enumerate(RELATIONS):
            if dl == 0:
                act(which, k, None)
            else:
                act(which, k, dl)

    def start_halo(which, k, dl):
        if dl is None:
            halo_copy(which, k).start()
        else:
            @pl.when((lat < L - 1) if dl == 1 else (lat > 0))
            def _():
                halo_copy(which, k).start()

    def recv_halo(which, k, dl):
        if dl is None:
            halo_copy(which, k).wait_recv()
        else:
            @pl.when((lat > 0) if dl == 1 else (lat < L - 1))
            def _():
                halo_copy(which, k).wait_recv()

    def sent_halo(which, k, dl):
        if dl is None:
            halo_copy(which, k).wait_send()
        else:
            @pl.when((lat < L - 1) if dl == 1 else (lat > 0))
            def _():
                halo_copy(which, k).wait_send()

    halo_each(0, start_halo)
    halo_each(1, start_halo)

    @pl.when(lat == 0)
    def _():
        for ref in (xn, xnw, xne, gn, gnw, gne):
            ref[...] = jnp.zeros(ref.shape, BF16)

    @pl.when(lat == L - 1)
    def _():
        for ref in (xs, xsw, xse, gs, gsw, gse):
            ref[...] = jnp.zeros(ref.shape, BF16)

    loads[0].wait()
    for ly in range(2):
        for k in range(9):
            wt[ly, k * C:(k + 1) * C, :] = wv[ly, k * C:(k + 1) * C, :].T
    loads[1].wait()
    loads[2].wait()
    loads[3].wait()
    halo_each(0, recv_halo)

    def assemble(n, nw, ne, mid_, w, e, s, sw, se):
        def band(a, b, c):
            return jnp.concatenate([a[...].astype(F32), b[...].astype(F32), c[...].astype(F32)], axis=1)
        whole = jnp.concatenate([band(nw, n, ne), band(w, mid_, e), band(sw, s, se)], axis=0)
        return whole.reshape(whole.shape[0] * WP, C)

    def put(ref, field, forward):
        for q, part_ in enumerate(triple(field, forward)):
            ref[:, q * C:(q + 1) * C] = part_

    def window(ref, starts, rows):
        return jnp.concatenate([ref[s * WP:(s + rows) * WP, :] for s in starts], axis=1)

    def clear(ref, first, rows, total):
        @pl.when(lat == 0)
        def _():
            ref[0:rows * WP, :] = jnp.zeros((rows * WP, 3 * C), BF16)

        @pl.when(lat == L - 1)
        def _():
            ref[(total - rows) * WP:total * WP, :] = jnp.zeros((rows * WP, 3 * C), BF16)

    put(x3, assemble(xn, xnw, xne, xin, xw, xe, xs, xsw, xse), True)
    R1, R2, R3 = H + 6, H + 4, H + 2
    z1 = jnp.dot(window(x3, (0, 1, 2), R1), wv[0], preferred_element_type=F32) + b_ref[0:1, :]
    sig = jax.nn.sigmoid(z1)
    s1[...] = slope(z1, sig)[2 * WP:(2 + R3) * WP, :]
    put(a3, z1 * sig, True)
    clear(a3, 0, 3, R1)

    halo_each(1, recv_halo)
    z2 = jnp.dot(window(a3, (0, 1, 2), R2), wv[1], preferred_element_type=F32) + b_ref[1:2, :]
    up = assemble(gn, gnw, gne, gin_buf, gw, ge, gs, gsw, gse)
    g2 = (up * slope(z2, jax.nn.sigmoid(z2)))
    put(g3, g2, False)

    column = lax.rem(lax.broadcasted_iota(jnp.int32, (H * WP, C), 0), WP)
    inside = (column >= PAD) & (column < PAD + W)

    def grads(field, start, first, ly, brow):
        own = jnp.where(inside, field[first * WP:(first + H) * WP, :].astype(BF16).astype(F32), 0.0)
        bsum = jnp.sum(own, axis=0, keepdims=True)
        bpart[lat, brow * 8:brow * 8 + 8, :] = jnp.broadcast_to(bsum, (8, C))
        flipped = own.astype(BF16).T
        ref = a3 if ly else x3
        for p in range(3):
            block = ref[(start + p) * WP:(start + p + H) * WP, :]
            three = jnp.dot(flipped, block, preferred_element_type=F32).astype(BF16)
            for q in range(3):
                yield three[:, q * C:(q + 1) * C].T

    def store_part(ly, blocks):
        whole = jnp.concatenate([v.astype(F32) for v in blocks], axis=0)
        extra = used * S - whole.shape[0]
        if extra:
            whole = jnp.concatenate([whole, jnp.zeros((extra, C), F32)], axis=0)
        for i in range(L * N):
            value = whole[i * S:(i + 1) * S].astype(BF16) if i < used else jnp.zeros((S, C), BF16)
            part[ly, i // (L2 * N), i // N % L2, i % N] = value

    def copy_to(src, dst, at, ly, peer):
        return pltpu.make_async_remote_copy(
            src_ref=src, dst_ref=dst, send_sem=red_send.at[ly, at], recv_sem=red_recv.at[ly, at],
            device_id=(seg,) + peer, device_id_type=MESH)

    def lat_copies(src_of, dst_of, base, ly):
        out, inc = [], []
        for d in range(1, L):
            to, frm = lat_peer(d), lat_peer(L - d)
            out.append(copy_to(src_of(to), dst_of(lat), base + d - 1, ly, (to, lon)))
            inc.append(copy_to(src_of(frm), dst_of(frm), base + d - 1, ly, (to, lon)))
        return out, inc

    def lon_copies(src_of, dst_of, base, ly):
        out, inc = [], []
        for d in range(1, N):
            to, frm = lon_peer(d), lon_peer(N - d)
            out.append(copy_to(src_of(to), dst_of(lon), base + d - 1, ly, (lat, to)))
            inc.append(copy_to(src_of(frm), dst_of(frm), base + d - 1, ly, (lat, to)))
        return out, inc

    pending = []

    def launch(pair):
        for c in pair[0]:
            c.start()
        pending.extend(pair[0])
        return pair[1]

    def arrive(incoming):
        for c in incoming:
            c.wait_recv()

    core, y = lax.rem(lat, 2), lat // 2
    partner = 2 * y + 1 - core

    def y_copies(src_of, dst_of, base, ly):
        out, inc = [], []
        for d in range(1, L2):
            to, frm = lax.rem(y + d, L2), lax.rem(y + L2 - d, L2)
            peer = (2 * to + core, lon)
            out.append(copy_to(src_of(to), dst_of(y), base + d - 1, ly, peer))
            inc.append(copy_to(src_of(frm), dst_of(frm), base + d - 1, ly, peer))
        return out, inc

    def y_slot(d):
        return lax.rem(y + d, L2)

    RSY, RSZ, AGZ, AGY, AGC = 1, 1 + L2, 1 + L2 + N, 1 + L2 + 2 * N, 1 + 2 * L2 + 2 * N

    def rs_core(ly):
        c = copy_to(part.at[ly, 1 - core], rc.at[ly], 0, ly, (partner, lon))
        return launch(([c], [c]))

    def rs_y(ly, incoming):
        arrive(incoming)
        m1[ly] = (part[ly, core].astype(F32) + rc[ly].astype(F32)).astype(BF16)
        return launch(y_copies(lambda to: m1.at[ly, to], lambda frm: rl.at[ly, frm], RSY, ly))

    def rs_lon(ly, incoming):
        arrive(incoming)
        total = m1[ly, y].astype(F32)
        for d in range(1, L2):
            total = total + rl[ly, y_slot(d)].astype(F32)
        mid[ly] = total.astype(BF16)
        return launch(lon_copies(lambda to: mid.at[ly, to], lambda frm: rn.at[ly, frm], RSZ, ly))

    def ag_lon(ly, incoming):
        arrive(incoming)
        total = mid[ly, lon].astype(F32)
        for d in range(1, N):
            total = total + rn[ly, lon_peer(d)].astype(F32)
        wout[ly, core, y, lon] = (total * scale).astype(BF16)
        return launch(lon_copies(lambda to: wout.at[ly, core, y, lon],
                                 lambda frm: wout.at[ly, core, y, frm], AGZ, ly))

    def core_copy(ly, d):
        out = copy_to(wout.at[ly, core, y_slot(d)], wout.at[ly, core, y_slot(d)], AGC + d, ly, (partner, lon))
        inc = copy_to(wout.at[ly, core, y_slot(d)], wout.at[ly, 1 - core, y_slot(d)], AGC + d, ly, (partner, lon))
        return [out], [inc]

    def ag_y(ly, incoming):
        arrive(incoming)
        other = launch(y_copies(lambda to: wout.at[ly, core, y], lambda frm: wout.at[ly, core, frm], AGY, ly))
        return other, launch(core_copy(ly, 0))

    def ag_core(ly, incoming):
        others, last = incoming
        for d in range(1, L2):
            arrive([others[L2 - d - 1]])
            last = last + launch(core_copy(ly, d))
        return last

    store_part(1, grads(g2, 2, 2, 1, 1))
    inc2 = rs_core(1)

    h1 = lax.dot_general(window(g3, (2, 1, 0), R3), wt[1], (((1,), (0,)), ((), ())),
                         preferred_element_type=F32)
    g1 = h1 * s1[...]
    put(p3, g1, False)
    clear(p3, 0, 1, R3)
    inc2 = rs_y(1, inc2)

    store_part(0, grads(g1, 3, 1, 0, 0))
    inc1 = rs_core(0)
    binc = launch(lat_copies(lambda to: bpart.at[lat], lambda frm: bpart.at[frm], 0, 2))
    inc1 = rs_y(0, inc1)
    inc2 = rs_lon(1, inc2)

    gi = jnp.dot(window(p3, (2, 1, 0), H), wt[0], preferred_element_type=F32)
    gi = gi.reshape(H, WP, C)[:, PAD:PAD + W, :]
    gin[...] = gi.astype(BF16)
    rows = gi.reshape(H // 2, 2, W, C)
    pool32[...] = (rows[:, 0] + rows[:, 1]).reshape(H // 2 * W, C)
    half = H // 2 * W // 2
    pool[...] = (pool32[pl.ds(0, half, stride=2), :] + pool32[pl.ds(1, half, stride=2), :]).astype(BF16)

    def skip_copy(to):
        return pltpu.make_async_remote_copy(
            src_ref=pool, dst_ref=skip_in, send_sem=skip_send, recv_sem=skip_recv,
            device_id=(to, lat, lon), device_id_type=MESH)

    @pl.when(seg > 0)
    def _():
        skip_copy(seg - 1).start()

    inc1 = rs_lon(0, inc1)
    inc2 = ag_lon(1, inc2)
    arrive(binc)
    total = bpart[0]
    for i in range(1, L):
        total = total + bpart[i]
    bmid[lon] = total
    binc = launch(lon_copies(lambda to: bmid.at[lon], lambda frm: bmid.at[frm], L, 2))
    inc1 = ag_lon(0, inc1)
    inc2 = ag_y(1, inc2)
    inc1 = ag_y(0, inc1)
    inc2 = ag_core(1, inc2)
    inc1 = ag_core(0, inc1)
    arrive(binc)
    total = bmid[0]
    for i in range(1, N):
        total = total + bmid[i]
    bout[...] = jnp.concatenate([total[0:1], total[8:9]], axis=0) * scale

    @pl.when(seg < nseg - 1)
    def _():
        skip_copy(seg).wait_recv()
        skip[...] = skip_in[...]

    @pl.when(seg == nseg - 1)
    def _():
        skip[...] = jnp.zeros(skip.shape, BF16)

    arrive(inc2)
    arrive(inc1)
    for c in pending:
        c.wait_send()
    halo_each(0, sent_halo)
    halo_each(1, sent_halo)

    @pl.when(seg > 0)
    def _():
        skip_copy(seg - 1).wait_send()


def finish(rows, w_ref, b_ref, gin_ref, skip_ref, w_out, b_out, gin_out, skip_out, wide, sem):
    copies = [pltpu.make_async_copy(gin_ref, gin_out, sem.at[0]),
              pltpu.make_async_copy(b_ref, b_out, sem.at[1]),
              pltpu.make_async_copy(skip_ref, skip_out, sem.at[2])]
    for copy in copies:
        copy.start()
    for ly in range(2):
        flat = w_ref[ly].reshape(-1, w_ref.shape[-1])
        wide[ly] = flat[:rows].astype(F32)
        copy = pltpu.make_async_copy(wide.at[ly], w_out.at[ly], sem.at[3 + ly])
        copy.start()
        copies.append(copy)
    for copy in copies:
        copy.wait()


def body(mesh_sizes, segment_input, weights, biases, out_grad):
    nseg, L, N = mesh_sizes
    _, H, W, C = segment_input.shape
    total_rows = 9 * C
    S = 8 * (-(-total_rows // (8 * L * N)))
    used = -(-total_rows // S)
    scale = 1.0 / math.sqrt(H * L * W * N)
    WP = W + 2 * PAD
    sizes = (nseg, L, N, H, W, C, S, used, scale)
    VM = pltpu.VMEM
    halos = []
    for rows in (XROWS, GROWS):
        halos += [VM((rows, W, C), BF16)] * 2 + [VM((H, PAD, C), BF16)] * 2 + [VM((rows, PAD, C), BF16)] * 4
    dma = pltpu.SemaphoreType.DMA
    per = 2 * (L + N) + 2
    vmem = pl.BlockSpec(memory_space=pltpu.VMEM)
    anyspace = pl.BlockSpec(memory_space=pl.ANY)
    hbm = pl.BlockSpec(memory_space=pltpu.HBM)
    half = H // 2 * W // 2
    finish_bytes = 2 * total_rows * C * 4 + (1 << 20)

    def in_hbm(array):
        return pltpu.with_memory_space_constraint(array, pltpu.HBM)

    wout, bout, gin, skip = pl.pallas_call(
        functools.partial(kernel, sizes),
        out_shape=(
            VM((2, 2, L // 2, N, S, C), BF16),
            VM((2, C), F32),
            VM((H, W, C), BF16),
            VM((half, C), BF16),
        ),
        in_specs=[hbm, hbm, hbm, hbm],
        out_specs=(vmem, vmem, vmem, vmem),
        scratch_shapes=[
            VM((H, W, C), BF16), VM((H, W, C), BF16), VM((2, C), F32),
            VM((2, 9 * C, C), BF16), VM((2, 9 * C, C), BF16),
            *halos,
            VM(((H + 8) * WP, 3 * C), BF16), VM(((H + 6) * WP, 3 * C), BF16),
            VM(((H + 4) * WP, 3 * C), BF16), VM(((H + 2) * WP, 3 * C), BF16),
            VM(((H + 2) * WP, C), F32),
            VM((2, 2, L // 2, N, S, C), BF16), *[VM((2, L // 2, N, S, C), BF16)] * 3,
            VM((2, N, S, C), BF16), VM((2, N, S, C), BF16),
            VM((L, 16, C), F32), VM((N, 16, C), F32),
            VM((H // 2 * W, C), F32), VM((H // 2 * W // 2, C), BF16), VM((H // 2 * W // 2, C), BF16),
            dma((4,)), dma((16,)), dma((16,)), dma((3, per)), dma((3, per)), dma(()), dma(()),
        ],
        compiler_params=pltpu.CompilerParams(collective_id=0, has_side_effects=True,
                                             vmem_limit_bytes=48 << 20),
    )(in_hbm(segment_input[0]), in_hbm(weights[0].reshape(2, 9 * C, C)), in_hbm(biases[0]), in_hbm(out_grad[0]))
    weight_grad, bias_grad, gin, skip = pl.pallas_call(
        functools.partial(finish, total_rows),
        out_shape=(
            jax.ShapeDtypeStruct((2, total_rows, C), F32),
            jax.ShapeDtypeStruct((2, C), F32),
            jax.ShapeDtypeStruct((H, W, C), BF16),
            jax.ShapeDtypeStruct((half, C), BF16),
        ),
        in_specs=[vmem] * 4,
        out_specs=(anyspace,) * 4,
        scratch_shapes=[VM((2, total_rows, C), F32), dma((5,))],
        compiler_params=pltpu.CompilerParams(vmem_limit_bytes=finish_bytes),
    )(wout, bout, gin, skip)
    return (weight_grad.reshape(1, 2, 3, 3, C, C), bias_grad[None], gin[None],
            skip.reshape(1, H // 2, W // 2, C))


def solution(mesh):
    placed = (
        P("segment", "lat", "lon", None),
        P("segment", None, None, None, None, None),
        P("segment", None, None),
        P("segment", "lat", "lon", None),
    )
    mesh_sizes = (mesh.shape["segment"], mesh.shape["lat"], mesh.shape["lon"])
    return jax.shard_map(
        functools.partial(body, mesh_sizes),
        mesh=mesh,
        in_specs=placed,
        out_specs=(
            P("segment", None, None, None, None, None),
            P("segment", None, None),
            P("segment", "lat", "lon", None),
            P("segment", "lat", "lon", None),
        ),
        check_vma=False,
    )
```

```python
import functools
import math

import jax
import jax.numpy as jnp
from jax import lax
from jax.experimental import pallas as pl
from jax.experimental.pallas import tpu as pltpu
from jax.sharding import PartitionSpec as P

MESH = pl.DeviceIdType.MESH
F32 = jnp.float32
BF16 = jnp.bfloat16
PAD = 8
XROWS = 4
GROWS = 2
GROUPS = 4
RELATIONS = ((1, 0), (-1, 0), (0, 1), (0, -1), (1, 1), (1, -1), (-1, 1), (-1, -1))


def triple(field, forward):
    count = field.shape[0]
    before = pltpu.roll(field, 1, 0).astype(BF16)
    after = pltpu.roll(field, count - 1, 0).astype(BF16)
    if forward:
        return before, field.astype(BF16), after
    return after, field.astype(BF16), before


def slope(value, sig):
    return sig * (1.0 + value * (1.0 - sig))


def kernel(sizes, x_hbm, w_hbm, b_hbm, g_hbm,
           wout, bout, gin, skip,
           xin, gin_buf, b_ref, wv, wt,
           xn, xs, xw, xe, xnw, xne, xsw, xse,
           gn, gs, gw, ge, gnw, gne, gsw, gse,
           x3, a3, g3, p3, s1,
           part, rc, m1, rl, mid, rn, bpart, bmid,
           pool32, pool, skip_in,
           local_sem, halo_send, halo_recv, red_send, red_recv, skip_send, skip_recv):
    nseg, L, N, H, W, C, S, used, scale, G = sizes
    WP, L2 = W + 2 * PAD, L // 2
    seg, lat, lon = lax.axis_index("segment"), lax.axis_index("lat"), lax.axis_index("lon")

    loads = [
        pltpu.make_async_copy(w_hbm, wv, local_sem.at[0]),
        pltpu.make_async_copy(x_hbm, xin, local_sem.at[1]),
        pltpu.make_async_copy(g_hbm, gin_buf, local_sem.at[2]),
        pltpu.make_async_copy(b_hbm, b_ref, local_sem.at[3]),
    ]
    for load in loads:
        load.start()

    def lat_peer(d):
        return lax.rem(lat + d, L)

    def lon_peer(d):
        return lax.rem(lon + (d + N), N)

    barrier = pltpu.get_barrier_semaphore()

    def greet(s, a, o):
        pl.semaphore_signal(barrier, inc=1, device_id=(s, a, o), device_id_type=MESH)

    for d in range(1, L):
        greet(seg, lat_peer(d), lon)
    for d in range(1, N):
        greet(seg, lat, lon_peer(d))

    @pl.when(lat > 0)
    def _():
        greet(seg, lat - 1, lon_peer(1))
        greet(seg, lat - 1, lon_peer(-1))

    @pl.when(lat < L - 1)
    def _():
        greet(seg, lat + 1, lon_peer(1))
        greet(seg, lat + 1, lon_peer(-1))

    @pl.when(seg > 0)
    def _():
        greet(seg - 1, lat, lon)

    @pl.when(seg < nseg - 1)
    def _():
        greet(seg + 1, lat, lon)

    def flag(condition):
        return lax.convert_element_type(condition, jnp.int32)

    peers = (L - 1 + N - 1 + 2 * flag(lat > 0) + 2 * flag(lat < L - 1)
             + flag(seg > 0) + flag(seg < nseg - 1))
    pl.semaphore_wait(barrier, peers)

    xdst = {(1, 0): xn, (-1, 0): xs, (0, 1): xw, (0, -1): xe,
            (1, 1): xnw, (1, -1): xne, (-1, 1): xsw, (-1, -1): xse}
    gdst = {(1, 0): gn, (-1, 0): gs, (0, 1): gw, (0, -1): ge,
            (1, 1): gnw, (1, -1): gne, (-1, 1): gsw, (-1, -1): gse}

    def piece(ref, rows, dl, do):
        r = {1: pl.ds(H - rows, rows), -1: pl.ds(0, rows), 0: pl.ds(0, H)}[dl]
        c = {1: pl.ds(W - PAD, PAD), -1: pl.ds(0, PAD), 0: pl.ds(0, W)}[do]
        return ref.at[r, c]

    def halo_copy(which, k):
        dl, do = RELATIONS[k]
        ref, rows, dst = (x_hbm, XROWS, xdst) if which == 0 else (g_hbm, GROWS, gdst)
        at = which * len(RELATIONS) + k
        return pltpu.make_async_remote_copy(
            src_ref=piece(ref, rows, dl, do),
            dst_ref=dst[(dl, do)],
            send_sem=halo_send.at[at],
            recv_sem=halo_recv.at[at],
            device_id=(seg, lat + dl, lon_peer(do)),
            device_id_type=MESH,
        )

    def halo_each(which, act):
        for k, (dl, do) in enumerate(RELATIONS):
            if dl == 0:
                act(which, k, None)
            else:
                act(which, k, dl)

    def start_halo(which, k, dl):
        if dl is None:
            halo_copy(which, k).start()
        else:
            @pl.when((lat < L - 1) if dl == 1 else (lat > 0))
            def _():
                halo_copy(which, k).start()

    def recv_halo(which, k, dl):
        if dl is None:
            halo_copy(which, k).wait_recv()
        else:
            @pl.when((lat > 0) if dl == 1 else (lat < L - 1))
            def _():
                halo_copy(which, k).wait_recv()

    def sent_halo(which, k, dl):
        if dl is None:
            halo_copy(which, k).wait_send()
        else:
            @pl.when((lat < L - 1) if dl == 1 else (lat > 0))
            def _():
                halo_copy(which, k).wait_send()

    halo_each(0, start_halo)
    halo_each(1, start_halo)

    @pl.when(lat == 0)
    def _():
        for ref in (xn, xnw, xne, gn, gnw, gne):
            ref[...] = jnp.zeros(ref.shape, BF16)

    @pl.when(lat == L - 1)
    def _():
        for ref in (xs, xsw, xse, gs, gsw, gse):
            ref[...] = jnp.zeros(ref.shape, BF16)

    loads[0].wait()
    for ly in range(2):
        for k in range(9):
            wt[ly, k * C:(k + 1) * C, :] = wv[ly, k * C:(k + 1) * C, :].T
    loads[1].wait()
    loads[2].wait()
    loads[3].wait()
    halo_each(0, recv_halo)

    def assemble(n, nw, ne, mid_, w, e, s, sw, se):
        def band(a, b, c):
            return jnp.concatenate([a[...].astype(F32), b[...].astype(F32), c[...].astype(F32)], axis=1)
        whole = jnp.concatenate([band(nw, n, ne), band(w, mid_, e), band(sw, s, se)], axis=0)
        return whole.reshape(whole.shape[0] * WP, C)

    def put(ref, field, forward):
        for q, part_ in enumerate(triple(field, forward)):
            ref[:, q * C:(q + 1) * C] = part_

    def window(ref, starts, rows):
        return jnp.concatenate([ref[s * WP:(s + rows) * WP, :] for s in starts], axis=1)

    def clear(ref, first, rows, total):
        @pl.when(lat == 0)
        def _():
            ref[0:rows * WP, :] = jnp.zeros((rows * WP, 3 * C), BF16)

        @pl.when(lat == L - 1)
        def _():
            ref[(total - rows) * WP:total * WP, :] = jnp.zeros((rows * WP, 3 * C), BF16)

    put(x3, assemble(xn, xnw, xne, xin, xw, xe, xs, xsw, xse), True)
    R1, R2, R3 = H + 6, H + 4, H + 2
    z1 = jnp.dot(window(x3, (0, 1, 2), R1), wv[0], preferred_element_type=F32) + b_ref[0:1, :]
    sig = jax.nn.sigmoid(z1)
    s1[...] = slope(z1, sig)[2 * WP:(2 + R3) * WP, :]
    put(a3, z1 * sig, True)
    clear(a3, 0, 3, R1)

    halo_each(1, recv_halo)
    z2 = jnp.dot(window(a3, (0, 1, 2), R2), wv[1], preferred_element_type=F32) + b_ref[1:2, :]
    up = assemble(gn, gnw, gne, gin_buf, gw, ge, gs, gsw, gse)
    g2 = (up * slope(z2, jax.nn.sigmoid(z2)))
    put(g3, g2, False)

    column = lax.rem(lax.broadcasted_iota(jnp.int32, (H * WP, C), 0), WP)
    inside = (column >= PAD) & (column < PAD + W)

    def grads(field, start, first, ly, brow):
        own = jnp.where(inside, field[first * WP:(first + H) * WP, :].astype(BF16).astype(F32), 0.0)
        bsum = jnp.sum(own, axis=0, keepdims=True)
        bpart[lat, brow * 8:brow * 8 + 8, :] = jnp.broadcast_to(bsum, (8, C))
        flipped = own.astype(BF16).T
        ref = a3 if ly else x3
        for p in range(3):
            block = ref[(start + p) * WP:(start + p + H) * WP, :]
            three = jnp.dot(flipped, block, preferred_element_type=F32).astype(BF16)
            for q in range(3):
                yield three[:, q * C:(q + 1) * C].T

    def store_part(ly, blocks):
        whole = jnp.concatenate([v.astype(F32) for v in blocks], axis=0)
        extra = used * S - whole.shape[0]
        if extra:
            whole = jnp.concatenate([whole, jnp.zeros((extra, C), F32)], axis=0)
        for i in range(L * N):
            value = whole[i * S:(i + 1) * S].astype(BF16) if i < used else jnp.zeros((S, C), BF16)
            part[ly, i // (L2 * N), i // N % L2, i % N] = value

    def copy_to(src, dst, at, ly, peer):
        return pltpu.make_async_remote_copy(
            src_ref=src, dst_ref=dst, send_sem=red_send.at[ly, at], recv_sem=red_recv.at[ly, at],
            device_id=(seg,) + peer, device_id_type=MESH)

    def lat_copies(src_of, dst_of, base, ly):
        out, inc = [], []
        for d in range(1, L):
            to, frm = lat_peer(d), lat_peer(L - d)
            out.append(copy_to(src_of(to), dst_of(lat), base + d - 1, ly, (to, lon)))
            inc.append(copy_to(src_of(frm), dst_of(frm), base + d - 1, ly, (to, lon)))
        return out, inc

    def lon_copies(src_of, dst_of, base, ly):
        out, inc = [], []
        for d in range(1, N):
            to, frm = lon_peer(d), lon_peer(N - d)
            out.append(copy_to(src_of(to), dst_of(lon), base + d - 1, ly, (lat, to)))
            inc.append(copy_to(src_of(frm), dst_of(frm), base + d - 1, ly, (lat, to)))
        return out, inc

    pending = []

    def launch(pair):
        for c in pair[0]:
            c.start()
        pending.extend(pair[0])
        return pair[1]

    def arrive(incoming):
        for c in incoming:
            c.wait_recv()

    core, y = lax.rem(lat, 2), lat // 2
    partner = (2 * y + 1 - core, lon)
    Z = N // G
    own = lon // Z
    low = 2 * lon < N
    mirrored = jnp.where(low, own, G - 1 - own)

    def near(k):
        if k == 0:
            return own
        at = k - 1 + jnp.where(k - 1 >= mirrored, 1, 0)
        return jnp.where(low, at, G - 1 - at)

    def zs(k):
        return pl.ds(near(k) * Z, Z)

    def y_to(d):
        return lax.rem(y + d, L2)

    def y_peer(d):
        return (2 * y_to(d) + core, lon)

    CRS, YRS = 0, G
    ZRS = YRS + (L2 - 1) * G
    ZAG = ZRS + N
    YAG = ZAG + N
    CAG = YAG + (L2 - 1) * G

    def send(src, dst, at, ly, peer):
        c = copy_to(src, dst, at, ly, peer)
        c.start()
        pending.append(c)

    def rs_core(ly):
        for k in reversed(range(G)):
            send(part.at[ly, 1 - core, :, zs(k)], rc.at[ly, :, zs(k)], CRS + k, ly, partner)

    def rs_y(ly, k):
        copy_to(part.at[ly, 1 - core, :, zs(k)], rc.at[ly, :, zs(k)], CRS + k, ly, partner).wait_recv()
        m1[ly, :, zs(k)] = (part[ly, core, :, zs(k)].astype(F32) + rc[ly, :, zs(k)].astype(F32)).astype(BF16)
        for d in range(1, L2):
            send(m1.at[ly, y_to(d), zs(k)], rl.at[ly, y, zs(k)], YRS + (d - 1) * G + k, ly, y_peer(d))

    def z_far(base, src_of, dst, ly, k, away):
        for j in reversed(range(Z)):
            t = near(k) * Z + j
            away(t, copy_to(src_of(t), dst, base + lax.rem(t - lon + N, N), ly, (lat, t)))

    def z_start(t, c):
        @pl.when(t != lon)
        def _():
            c.start()

    def z_sent(t, c):
        @pl.when(t != lon)
        def _():
            c.wait_send()

    def rs_z(ly, k, act=z_start):
        if act is z_start:
            total = m1[ly, y, zs(k)].astype(F32)
            for d in range(1, L2):
                frm = y_to(L2 - d)
                copy_to(m1.at[ly, frm, zs(k)], rl.at[ly, frm, zs(k)], YRS + (d - 1) * G + k, ly,
                        y_peer(d)).wait_recv()
                total = total + rl[ly, frm, zs(k)].astype(F32)
            mid[ly, zs(k)] = total.astype(BF16)
        z_far(ZRS, lambda t: mid.at[ly, t], rn.at[ly, lon], ly, k, act)

    def z_wait(src, dst_of, base, ly, frm):
        copy_to(src, dst_of(frm), base + lax.rem(lon - frm + N, N), ly, (lat, frm)).wait_recv()

    def total_z(ly):
        total = mid[ly, lon].astype(F32)
        for d in range(1, N):
            frm = lon_peer(d)
            z_wait(mid.at[ly, frm], lambda i: rn.at[ly, i], ZRS, ly, frm)
        for d in range(1, N):
            total = total + rn[ly, lon_peer(d)].astype(F32)
        wout[ly, core, y, lon] = (total * scale).astype(BF16)
        for k in reversed(range(G)):
            ag_z(ly, k, z_start)

    def ag_z(ly, k, act):
        z_far(ZAG, lambda t: wout.at[ly, core, y, lon], wout.at[ly, core, y, lon], ly, k, act)

    def forward(ly, k):
        for j in range(Z):
            frm = near(k) * Z + j

            @pl.when(frm != lon)
            def _():
                z_wait(wout.at[ly, core, y, lon], lambda i: wout.at[ly, core, y, i], ZAG, ly, frm)

        piece = wout.at[ly, core, y, zs(k)]
        for d in range(1, L2):
            send(piece, piece, YAG + (d - 1) * G + k, ly, y_peer(d))
        send(piece, piece, CAG + k, ly, partner)

    def forward_y(ly, k):
        for d in range(1, L2):
            piece = wout.at[ly, core, y_to(L2 - d), zs(k)]
            copy_to(wout.at[ly, core, y, zs(k)], piece, YAG + (d - 1) * G + k, ly, y_peer(d)).wait_recv()
            send(piece, piece, CAG + d * G + k, ly, partner)

    def settle(ly):
        for k in range(G):
            for d in range(L2):
                at = y_to(L2 - d) if d else y
                copy_to(wout.at[ly, core, at, zs(k)], wout.at[ly, 1 - core, at, zs(k)], CAG + d * G + k, ly,
                        partner).wait_recv()
            rs_z(ly, k, z_sent)
            ag_z(ly, k, z_sent)

    store_part(1, grads(g2, 2, 2, 1, 1))
    rs_core(1)

    h1 = lax.dot_general(window(g3, (2, 1, 0), R3), wt[1], (((1,), (0,)), ((), ())),
                         preferred_element_type=F32)
    g1 = h1 * s1[...]
    put(p3, g1, False)
    clear(p3, 0, 1, R3)
    for k in reversed(range(G)):
        rs_y(1, k)

    store_part(0, grads(g1, 3, 1, 0, 0))
    rs_core(0)
    binc = launch(lat_copies(lambda to: bpart.at[lat], lambda frm: bpart.at[frm], 0, 2))

    gi = jnp.dot(window(p3, (2, 1, 0), H), wt[0], preferred_element_type=F32)
    gi = gi.reshape(H, WP, C)[:, PAD:PAD + W, :]
    gin[...] = gi.astype(BF16)
    rows = gi.reshape(H // 2, 2, W, C)
    pool32[...] = (rows[:, 0] + rows[:, 1]).reshape(H // 2 * W, C)
    half = H // 2 * W // 2
    pool[...] = (pool32[pl.ds(0, half, stride=2), :] + pool32[pl.ds(1, half, stride=2), :]).astype(BF16)

    def skip_copy(to):
        return pltpu.make_async_remote_copy(
            src_ref=pool, dst_ref=skip_in, send_sem=skip_send, recv_sem=skip_recv,
            device_id=(to, lat, lon), device_id_type=MESH)

    for k in reversed(range(G)):
        rs_y(0, k)

    @pl.when(seg > 0)
    def _():
        skip_copy(seg - 1).start()

    for k in reversed(range(G)):
        rs_z(1, k)
    arrive(binc)
    total = bpart[0]
    for i in range(1, L):
        total = total + bpart[i]
    bmid[lon] = total
    binc = launch(lon_copies(lambda to: bmid.at[lon], lambda frm: bmid.at[frm], L, 2))
    for k in reversed(range(G)):
        rs_z(0, k)
    total_z(1)
    for k in range(G - 2):
        forward(1, k)
    total_z(0)
    forward(0, 0)
    for k in range(G - 2, G):
        forward(1, k)
    for k in range(G):
        forward_y(1, k)
    for k in range(1, G):
        forward(0, k)
    arrive(binc)
    total = bmid[0]
    for i in range(1, N):
        total = total + bmid[i]
    bout[...] = jnp.concatenate([total[0:1], total[8:9]], axis=0) * scale

    @pl.when(seg < nseg - 1)
    def _():
        skip_copy(seg).wait_recv()
        skip[...] = skip_in[...]

    @pl.when(seg == nseg - 1)
    def _():
        skip[...] = jnp.zeros(skip.shape, BF16)

    for k in range(G):
        forward_y(0, k)
    settle(1)
    settle(0)
    for c in pending:
        c.wait_send()
    halo_each(0, sent_halo)
    halo_each(1, sent_halo)

    @pl.when(seg > 0)
    def _():
        skip_copy(seg - 1).wait_send()


def finish(rows, w_ref, b_ref, gin_ref, skip_ref, w_out, b_out, gin_out, skip_out, wide, sem):
    copies = [pltpu.make_async_copy(gin_ref, gin_out, sem.at[0]),
              pltpu.make_async_copy(b_ref, b_out, sem.at[1]),
              pltpu.make_async_copy(skip_ref, skip_out, sem.at[2])]
    for copy in copies:
        copy.start()
    for ly in range(2):
        flat = w_ref[ly].reshape(-1, w_ref.shape[-1])
        wide[ly] = flat[:rows].astype(F32)
        copy = pltpu.make_async_copy(wide.at[ly], w_out.at[ly], sem.at[3 + ly])
        copy.start()
        copies.append(copy)
    for copy in copies:
        copy.wait()


def body(mesh_sizes, segment_input, weights, biases, out_grad):
    nseg, L, N = mesh_sizes
    _, H, W, C = segment_input.shape
    total_rows = 9 * C
    S = 8 * (-(-total_rows // (8 * L * N)))
    used = -(-total_rows // S)
    scale = 1.0 / math.sqrt(H * L * W * N)
    WP = W + 2 * PAD
    G = math.gcd(N, GROUPS)
    sizes = (nseg, L, N, H, W, C, S, used, scale, G)
    VM = pltpu.VMEM
    halos = []
    for rows in (XROWS, GROWS):
        halos += [VM((rows, W, C), BF16)] * 2 + [VM((H, PAD, C), BF16)] * 2 + [VM((rows, PAD, C), BF16)] * 4
    dma = pltpu.SemaphoreType.DMA
    per = max(L + N, G * (1 + 2 * (L // 2 - 1) + L // 2) + 2 * N)
    vmem = pl.BlockSpec(memory_space=pltpu.VMEM)
    anyspace = pl.BlockSpec(memory_space=pl.ANY)
    hbm = pl.BlockSpec(memory_space=pltpu.HBM)
    half = H // 2 * W // 2
    finish_bytes = 2 * total_rows * C * 4 + (1 << 20)

    def in_hbm(array):
        return pltpu.with_memory_space_constraint(array, pltpu.HBM)

    wout, bout, gin, skip = pl.pallas_call(
        functools.partial(kernel, sizes),
        out_shape=(
            VM((2, 2, L // 2, N, S, C), BF16),
            VM((2, C), F32),
            VM((H, W, C), BF16),
            VM((half, C), BF16),
        ),
        in_specs=[hbm, hbm, hbm, hbm],
        out_specs=(vmem, vmem, vmem, vmem),
        scratch_shapes=[
            VM((H, W, C), BF16), VM((H, W, C), BF16), VM((2, C), F32),
            VM((2, 9 * C, C), BF16), VM((2, 9 * C, C), BF16),
            *halos,
            VM(((H + 8) * WP, 3 * C), BF16), VM(((H + 6) * WP, 3 * C), BF16),
            VM(((H + 4) * WP, 3 * C), BF16), VM(((H + 2) * WP, 3 * C), BF16),
            VM(((H + 2) * WP, C), F32),
            VM((2, 2, L // 2, N, S, C), BF16), *[VM((2, L // 2, N, S, C), BF16)] * 3,
            VM((2, N, S, C), BF16), VM((2, N, S, C), BF16),
            VM((L, 16, C), F32), VM((N, 16, C), F32),
            VM((H // 2 * W, C), F32), VM((H // 2 * W // 2, C), BF16), VM((H // 2 * W // 2, C), BF16),
            dma((4,)), dma((16,)), dma((16,)), dma((3, per)), dma((3, per)), dma(()), dma(()),
        ],
        compiler_params=pltpu.CompilerParams(collective_id=0, has_side_effects=True,
                                             vmem_limit_bytes=48 << 20),
    )(in_hbm(segment_input[0]), in_hbm(weights[0].reshape(2, 9 * C, C)), in_hbm(biases[0]), in_hbm(out_grad[0]))
    weight_grad, bias_grad, gin, skip = pl.pallas_call(
        functools.partial(finish, total_rows),
        out_shape=(
            jax.ShapeDtypeStruct((2, total_rows, C), F32),
            jax.ShapeDtypeStruct((2, C), F32),
            jax.ShapeDtypeStruct((H, W, C), BF16),
            jax.ShapeDtypeStruct((half, C), BF16),
        ),
        in_specs=[vmem] * 4,
        out_specs=(anyspace,) * 4,
        scratch_shapes=[VM((2, total_rows, C), F32), dma((5,))],
        compiler_params=pltpu.CompilerParams(vmem_limit_bytes=finish_bytes),
    )(wout, bout, gin, skip)
    return (weight_grad.reshape(1, 2, 3, 3, C, C), bias_grad[None], gin[None],
            skip.reshape(1, H // 2, W // 2, C))


def solution(mesh):
    placed = (
        P("segment", "lat", "lon", None),
        P("segment", None, None, None, None, None),
        P("segment", None, None),
        P("segment", "lat", "lon", None),
    )
    mesh_sizes = (mesh.shape["segment"], mesh.shape["lat"], mesh.shape["lon"])
    return jax.shard_map(
        functools.partial(body, mesh_sizes),
        mesh=mesh,
        in_specs=placed,
        out_specs=(
            P("segment", None, None, None, None, None),
            P("segment", None, None),
            P("segment", "lat", "lon", None),
            P("segment", "lat", "lon", None),
        ),
        check_vma=False,
    )
```

```python
import functools
import math

import jax
import jax.numpy as jnp
from jax import lax
from jax.experimental import pallas as pl
from jax.experimental.pallas import tpu as pltpu
from jax.sharding import PartitionSpec as P

MESH = pl.DeviceIdType.MESH
F32 = jnp.float32
BF16 = jnp.bfloat16
PAD = 8
XROWS = 4
GROWS = 2
GROUPS = 4


def triple(field, forward):
    count = field.shape[0]
    before = pltpu.roll(field, 1, 0).astype(BF16)
    after = pltpu.roll(field, count - 1, 0).astype(BF16)
    if forward:
        return before, field.astype(BF16), after
    return after, field.astype(BF16), before


def gate(value):
    return 0.5 * jnp.tanh(0.5 * value) + 0.5


def slope(sig, act):
    return sig * (1.0 - act) + act


def kernel(sizes, x_hbm, w_hbm, b_hbm, g_hbm,
           wout, bout, gin, skip,
           xpad, gpad, b_ref, wv, wt,
           x3, a3, g3, p3, s1,
           part, rc, m1, rl, mid, rn, bpart, bmid,
           pool32, pool, skip_in,
           local_sem, halo_recv, red_recv, sent_sem):
    nseg, L, N, H, W, C, S, used, scale, G = sizes
    WP, L2 = W + 2 * PAD, L // 2
    seg, lat, lon = lax.axis_index("segment"), lax.axis_index("lat"), lax.axis_index("lon")

    loads = [
        pltpu.make_async_copy(w_hbm, wv, local_sem.at[0]),
        pltpu.make_async_copy(x_hbm, xpad.at[pl.ds(XROWS, H), pl.ds(PAD, W)], local_sem.at[1]),
        pltpu.make_async_copy(g_hbm, gpad.at[pl.ds(GROWS, H), pl.ds(PAD, W)], local_sem.at[2]),
        pltpu.make_async_copy(b_hbm, b_ref, local_sem.at[3]),
    ]
    for load in loads:
        load.start()

    def lat_peer(d):
        return lax.rem(lat + d, L)

    def lon_peer(d):
        return lax.rem(lon + (d + N), N)

    barrier = pltpu.get_barrier_semaphore()

    def greet(s, a, o):
        pl.semaphore_signal(barrier, inc=1, device_id=(s, a, o), device_id_type=MESH)

    for d in range(1, L):
        greet(seg, lat_peer(d), lon)
    for d in range(1, N):
        greet(seg, lat, lon_peer(d))

    @pl.when(lat > 0)
    def _():
        greet(seg, lat - 1, lon_peer(1))
        greet(seg, lat - 1, lon_peer(-1))

    @pl.when(lat < L - 1)
    def _():
        greet(seg, lat + 1, lon_peer(1))
        greet(seg, lat + 1, lon_peer(-1))

    @pl.when(seg > 0)
    def _():
        greet(seg - 1, lat, lon)

    @pl.when(seg < nseg - 1)
    def _():
        greet(seg + 1, lat, lon)

    def flag(condition):
        return lax.convert_element_type(condition, jnp.int32)

    peers = (L - 1 + N - 1 + 2 * flag(lat > 0) + 2 * flag(lat < L - 1)
             + flag(seg > 0) + flag(seg < nseg - 1))
    pl.semaphore_wait(barrier, peers)

    low = 2 * lon < N
    far = jnp.where(low, -1, 1)

    def halo_copy(which, dl, turn):
        ref, dst, rows = (x_hbm, xpad, XROWS) if which == 0 else (g_hbm, gpad, GROWS)
        r = {1: pl.ds(H - rows, rows), -1: pl.ds(0, rows), 0: pl.ds(0, H)}[dl]
        to_r = {1: pl.ds(0, rows), -1: pl.ds(rows + H, rows), 0: pl.ds(rows, H)}[dl]
        do = turn * far
        if turn == 0:
            c, to_c = pl.ds(0, W), pl.ds(PAD, W)
        else:
            c = pl.ds(pl.multiple_of(jnp.where(do > 0, W - PAD, 0), PAD), PAD)
            to_c = pl.ds(pl.multiple_of(jnp.where(do > 0, 0, W + PAD), PAD), PAD)
        return pltpu.make_async_remote_copy(
            src_ref=ref.at[r, c],
            dst_ref=dst.at[to_r, to_c],
            send_sem=sent_sem.at[0],
            recv_sem=halo_recv.at[which, dl % 3],
            device_id=(seg, lat + dl, lon_peer(do)),
            device_id_type=MESH,
        )

    def start_halo(which):
        for turn in (1, 0, -1):
            for dl in (1, -1, 0):
                if dl == 0:
                    if turn:
                        halo_copy(which, dl, turn).start()
                else:
                    @pl.when((lat < L - 1) if dl == 1 else (lat > 0))
                    def _():
                        halo_copy(which, dl, turn).start()

    def halo_whole(which, dl):
        dst, rows = (xpad, XROWS) if which == 0 else (gpad, GROWS)
        if dl == 0:
            region = dst.at[pl.ds(rows, H), pl.ds(0, 2 * PAD)]
        else:
            region = dst.at[pl.ds(0 if dl == 1 else rows + H, rows)]
        return pltpu.make_async_remote_copy(
            src_ref=region, dst_ref=region, send_sem=sent_sem.at[0], recv_sem=halo_recv.at[which, dl % 3],
            device_id=(seg, lat, lon_peer(1)), device_id_type=MESH)

    def recv_halo(which):
        @pl.when(lat > 0)
        def _():
            halo_whole(which, 1).wait_recv()

        @pl.when(lat < L - 1)
        def _():
            halo_whole(which, -1).wait_recv()
        halo_whole(which, 0).wait_recv()

    def sent_halo(which):
        @pl.when(lat < L - 1)
        def _():
            halo_whole(which, 1).wait_send()

        @pl.when(lat > 0)
        def _():
            halo_whole(which, -1).wait_send()
        halo_whole(which, 0).wait_send()

    start_halo(0)
    start_halo(1)

    @pl.when(lat == 0)
    def _():
        xpad[0:XROWS] = jnp.zeros((XROWS, WP, C), BF16)
        gpad[0:GROWS] = jnp.zeros((GROWS, WP, C), BF16)

    @pl.when(lat == L - 1)
    def _():
        xpad[XROWS + H:] = jnp.zeros((XROWS, WP, C), BF16)
        gpad[GROWS + H:] = jnp.zeros((GROWS, WP, C), BF16)

    loads[0].wait()
    for ly in range(2):
        for k in range(9):
            wt[ly, k * C:(k + 1) * C, :] = wv[ly, k * C:(k + 1) * C, :].T
    loads[1].wait()
    loads[2].wait()
    loads[3].wait()
    recv_halo(0)

    def put(ref, field, forward):
        for q, part_ in enumerate(triple(field, forward)):
            ref[:, q * C:(q + 1) * C] = part_

    def window(ref, starts, rows):
        return jnp.concatenate([ref[s * WP:(s + rows) * WP, :] for s in starts], axis=1)

    def clear(ref, first, rows, total):
        @pl.when(lat == 0)
        def _():
            ref[0:rows * WP, :] = jnp.zeros((rows * WP, 3 * C), BF16)

        @pl.when(lat == L - 1)
        def _():
            ref[(total - rows) * WP:total * WP, :] = jnp.zeros((rows * WP, 3 * C), BF16)

    put(x3, xpad[...].astype(F32).reshape((H + 2 * XROWS) * WP, C), True)
    R1, R2, R3 = H + 6, H + 4, H + 2
    z1 = jnp.dot(window(x3, (0, 1, 2), R1), wv[0], preferred_element_type=F32) + b_ref[0:1, :]
    sig = gate(z1)
    a1 = z1 * sig
    s1[...] = slope(sig, a1)[2 * WP:(2 + R3) * WP, :]
    put(a3, a1, True)
    clear(a3, 0, 3, R1)

    recv_halo(1)
    z2 = jnp.dot(window(a3, (0, 1, 2), R2), wv[1], preferred_element_type=F32) + b_ref[1:2, :]
    up = gpad[...].astype(F32).reshape((H + 2 * GROWS) * WP, C)
    sig = gate(z2)
    g2 = up * slope(sig, z2 * sig)
    put(g3, g2, False)

    column = lax.rem(lax.broadcasted_iota(jnp.int32, (H * WP, C), 0), WP)
    inside = (column >= PAD) & (column < PAD + W)

    def grads(field, start, first, ly, brow):
        own = jnp.where(inside, field[first * WP:(first + H) * WP, :].astype(BF16).astype(F32), 0.0)
        bsum = jnp.sum(own, axis=0, keepdims=True)
        bpart[lat, brow * 8:brow * 8 + 8, :] = jnp.broadcast_to(bsum, (8, C))
        flipped = own.astype(BF16).T
        ref = a3 if ly else x3
        for p in range(3):
            block = ref[(start + p) * WP:(start + p + H) * WP, :]
            three = jnp.dot(flipped, block, preferred_element_type=F32).astype(BF16)
            for q in range(3):
                yield three[:, q * C:(q + 1) * C].T

    def store_part(ly, blocks):
        whole = jnp.concatenate([v.astype(F32) for v in blocks], axis=0)
        extra = used * S - whole.shape[0]
        if extra:
            whole = jnp.concatenate([whole, jnp.zeros((extra, C), F32)], axis=0)
        for i in range(L * N):
            value = whole[i * S:(i + 1) * S].astype(BF16) if i < used else jnp.zeros((S, C), BF16)
            part[ly, i // (L2 * N), i // N % L2, i % N] = value

    core, y = lax.rem(lat, 2), lat // 2
    partner = (2 * y + 1 - core, lon)
    Z = N // G
    own = lon // Z
    mirrored = jnp.where(low, own, G - 1 - own)
    CRS, ZRS, YAG, CAG, YRS = 0, 1, 2, 3, 4
    ZAG = YRS + G
    pending = []

    def copy_to(src, dst, at, ly, peer):
        return pltpu.make_async_remote_copy(
            src_ref=src, dst_ref=dst, send_sem=sent_sem.at[0], recv_sem=red_recv.at[ly, at],
            device_id=(seg,) + peer, device_id_type=MESH)

    def arrived(region, at, ly):
        copy_to(region, region, at, ly, partner).wait_recv()

    def send(src, dst, at, ly, peer):
        copy_to(src, dst, at, ly, peer).start()
        pending.append(src)

    def near(k):
        if k == 0:
            return own
        at = k - 1 + jnp.where(k - 1 >= mirrored, 1, 0)
        return jnp.where(low, at, G - 1 - at)

    def zs(k):
        return pl.ds(near(k) * Z, Z)

    def y_to(d):
        return lax.rem(y + d, L2)

    def y_peer(d):
        return (2 * y_to(d) + core, lon)

    def rs_core(ly):
        send(part.at[ly, 1 - core], rc.at[ly], CRS, ly, partner)

    def rs_y(ly):
        arrived(rc.at[ly], CRS, ly)
        for k in reversed(range(G)):
            m1[ly, :, zs(k)] = (part[ly, core, :, zs(k)].astype(F32) + rc[ly, :, zs(k)].astype(F32)).astype(BF16)
            for d in range(1, L2):
                send(m1.at[ly, y_to(d), zs(k)], rl.at[ly, d - 1, zs(k)], YRS + k, ly, y_peer(d))

    def z_away(k, act):
        for j in reversed(range(Z)):
            t = near(k) * Z + j

            @pl.when(t != lon)
            def _():
                act(t, lax.rem(t - lon + N, N))

    def rs_z(ly, k):
        total = m1[ly, y, zs(k)].astype(F32)
        if L2 > 1:
            arrived(rl.at[ly, :, zs(k)], YRS + k, ly)
        for d in range(1, L2):
            total = total + rl[ly, L2 - d - 1, zs(k)].astype(F32)
        mid[ly, zs(k)] = total.astype(BF16)
        z_away(k, lambda t, d: copy_to(mid.at[ly, t], rn.at[ly, d - 1], ZRS, ly, (lat, t)).start())

    def total_z(ly):
        total = mid[ly, lon].astype(F32)
        arrived(rn.at[ly], ZRS, ly)
        for d in range(1, N):
            total = total + rn[ly, N - d - 1].astype(F32)
        wout[ly, core, y, lon] = (total * scale).astype(BF16)
        piece = wout.at[ly, core, y, lon]
        for k in reversed(range(G)):
            z_away(k, lambda t, d: copy_to(piece, piece, ZAG + d - 1, ly, (lat, t)).start())

    def forward(ly, k):
        for j in range(Z):
            frm = near(k) * Z + j

            @pl.when(frm != lon)
            def _():
                arrived(wout.at[ly, core, y, frm], ZAG + lax.rem(lon - frm + N, N) - 1, ly)

        piece = wout.at[ly, core, y, zs(k)]
        for d in range(1, L2):
            send(piece, piece, YAG, ly, y_peer(d))
        send(piece, piece, CAG, ly, partner)

    def forward_y(ly):
        for d in range(1, L2):
            arrived(wout.at[ly, core, y], YAG, ly)
        for d in range(1, L2):
            piece = wout.at[ly, core, y_to(d)]
            send(piece, piece, CAG, ly, partner)

    def settle(ly):
        arrived(wout.at[ly, 1 - core], CAG, ly)

    store_part(1, grads(g2, 2, 2, 1, 1))
    rs_core(1)

    h1 = lax.dot_general(window(g3, (2, 1, 0), R3), wt[1], (((1,), (0,)), ((), ())),
                         preferred_element_type=F32)
    g1 = h1 * s1[...]
    put(p3, g1, False)
    clear(p3, 0, 1, R3)
    rs_y(1)

    store_part(0, grads(g1, 3, 1, 0, 0))
    rs_core(0)
    for d in range(1, L):
        send(bpart.at[lat], bpart.at[lat], 0, 2, (lat_peer(d), lon))

    gi = jnp.dot(window(p3, (2, 1, 0), H), wt[0], preferred_element_type=F32)
    gi = gi.reshape(H, WP, C)[:, PAD:PAD + W, :]
    gin[...] = gi.astype(BF16)
    rows = gi.reshape(H // 2, 2, W, C)
    pool32[...] = (rows[:, 0] + rows[:, 1]).reshape(H // 2 * W, C)
    half = H // 2 * W // 2
    pool[...] = (pool32[pl.ds(0, half, stride=2), :] + pool32[pl.ds(1, half, stride=2), :]).astype(BF16)

    def skip_copy(to):
        return pltpu.make_async_remote_copy(
            src_ref=pool, dst_ref=skip_in, send_sem=sent_sem.at[0], recv_sem=red_recv.at[2, 2],
            device_id=(to, lat, lon), device_id_type=MESH)

    rs_y(0)

    @pl.when(seg > 0)
    def _():
        skip_copy(seg - 1).start()

    for k in reversed(range(G)):
        rs_z(1, k)
    arrived(bpart.at[pl.ds(0, L - 1)], 0, 2)
    total = bpart[0]
    for i in range(1, L):
        total = total + bpart[i]
    bmid[lon] = total
    for d in range(1, N):
        send(bmid.at[lon], bmid.at[lon], 1, 2, (lat, lon_peer(d)))
    for k in reversed(range(G)):
        rs_z(0, k)
    total_z(1)
    forward(1, 0)
    total_z(0)
    forward(0, 0)
    for k in range(1, G):
        forward(1, k)
    for k in range(1, G):
        forward(0, k)
    forward_y(1)
    arrived(bmid.at[pl.ds(0, N - 1)], 1, 2)
    total = bmid[0]
    for i in range(1, N):
        total = total + bmid[i]
    bout[...] = jnp.concatenate([total[0:1], total[8:9]], axis=0) * scale

    @pl.when(seg < nseg - 1)
    def _():
        skip_copy(seg).wait_recv()
        skip[...] = skip_in[...]

    @pl.when(seg == nseg - 1)
    def _():
        skip[...] = jnp.zeros(skip.shape, BF16)

    forward_y(0)
    settle(1)
    settle(0)
    for src in pending:
        copy_to(src, src, 0, 2, partner).wait_send()
    for ly in range(2):
        for ref in (mid, wout.at[:, core, y]):
            src = ref.at[ly, pl.ds(0, N - 1)]
            copy_to(src, src, 0, 2, partner).wait_send()
    sent_halo(0)
    sent_halo(1)

    @pl.when(seg > 0)
    def _():
        skip_copy(seg - 1).wait_send()


def finish(rows, w_ref, b_ref, gin_ref, skip_ref, w_out, b_out, gin_out, skip_out, wide, sem):
    copies = [pltpu.make_async_copy(gin_ref, gin_out, sem.at[0]),
              pltpu.make_async_copy(b_ref, b_out, sem.at[1]),
              pltpu.make_async_copy(skip_ref, skip_out, sem.at[2])]
    for copy in copies:
        copy.start()
    for ly in range(2):
        flat = w_ref[ly].reshape(-1, w_ref.shape[-1])
        wide[ly] = flat[:rows].astype(F32)
        copy = pltpu.make_async_copy(wide.at[ly], w_out.at[ly], sem.at[3 + ly])
        copy.start()
        copies.append(copy)
    for copy in copies:
        copy.wait()


def body(mesh_sizes, segment_input, weights, biases, out_grad):
    nseg, L, N = mesh_sizes
    _, H, W, C = segment_input.shape
    total_rows = 9 * C
    S = 8 * (-(-total_rows // (8 * L * N)))
    used = -(-total_rows // S)
    scale = 1.0 / math.sqrt(H * L * W * N)
    WP = W + 2 * PAD
    G = math.gcd(N, GROUPS)
    sizes = (nseg, L, N, H, W, C, S, used, scale, G)
    VM = pltpu.VMEM
    dma = pltpu.SemaphoreType.DMA
    per = 4 + G + N - 1
    vmem = pl.BlockSpec(memory_space=pltpu.VMEM)
    anyspace = pl.BlockSpec(memory_space=pl.ANY)
    hbm = pl.BlockSpec(memory_space=pltpu.HBM)
    half = H // 2 * W // 2
    finish_bytes = 2 * total_rows * C * 4 + (1 << 20)

    def in_hbm(array):
        return pltpu.with_memory_space_constraint(array, pltpu.HBM)

    wout, bout, gin, skip = pl.pallas_call(
        functools.partial(kernel, sizes),
        out_shape=(
            VM((2, 2, L // 2, N, S, C), BF16),
            VM((2, C), F32),
            VM((H, W, C), BF16),
            VM((half, C), BF16),
        ),
        in_specs=[hbm, hbm, hbm, hbm],
        out_specs=(vmem, vmem, vmem, vmem),
        scratch_shapes=[
            VM((H + 2 * XROWS, WP, C), BF16), VM((H + 2 * GROWS, WP, C), BF16), VM((2, C), F32),
            VM((2, 9 * C, C), BF16), VM((2, 9 * C, C), BF16),
            VM(((H + 8) * WP, 3 * C), BF16), VM(((H + 6) * WP, 3 * C), BF16),
            VM(((H + 4) * WP, 3 * C), BF16), VM(((H + 2) * WP, 3 * C), BF16),
            VM(((H + 2) * WP, C), F32),
            VM((2, 2, L // 2, N, S, C), BF16), VM((2, L // 2, N, S, C), BF16), VM((2, L // 2, N, S, C), BF16),
            VM((2, L // 2 - 1, N, S, C), BF16), VM((2, N, S, C), BF16), VM((2, N - 1, S, C), BF16),
            VM((L, 16, C), F32), VM((N, 16, C), F32),
            VM((H // 2 * W, C), F32), VM((H // 2 * W // 2, C), BF16), VM((H // 2 * W // 2, C), BF16),
            dma((4,)), dma((2, 3)), dma((3, per)), dma((1,)),
        ],
        compiler_params=pltpu.CompilerParams(collective_id=0, has_side_effects=True,
                                             vmem_limit_bytes=48 << 20),
    )(in_hbm(segment_input[0]), in_hbm(weights[0].reshape(2, 9 * C, C)), in_hbm(biases[0]), in_hbm(out_grad[0]))
    weight_grad, bias_grad, gin, skip = pl.pallas_call(
        functools.partial(finish, total_rows),
        out_shape=(
            jax.ShapeDtypeStruct((2, total_rows, C), F32),
            jax.ShapeDtypeStruct((2, C), F32),
            jax.ShapeDtypeStruct((H, W, C), BF16),
            jax.ShapeDtypeStruct((half, C), BF16),
        ),
        in_specs=[vmem] * 4,
        out_specs=(anyspace,) * 4,
        scratch_shapes=[VM((2, total_rows, C), F32), dma((5,))],
        compiler_params=pltpu.CompilerParams(vmem_limit_bytes=finish_bytes),
    )(wout, bout, gin, skip)
    return (weight_grad.reshape(1, 2, 3, 3, C, C), bias_grad[None], gin[None],
            skip.reshape(1, H // 2, W // 2, C))


def solution(mesh):
    placed = (
        P("segment", "lat", "lon", None),
        P("segment", None, None, None, None, None),
        P("segment", None, None),
        P("segment", "lat", "lon", None),
    )
    mesh_sizes = (mesh.shape["segment"], mesh.shape["lat"], mesh.shape["lon"])
    return jax.shard_map(
        functools.partial(body, mesh_sizes),
        mesh=mesh,
        in_specs=placed,
        out_specs=(
            P("segment", None, None, None, None, None),
            P("segment", None, None),
            P("segment", "lat", "lon", None),
            P("segment", "lat", "lon", None),
        ),
        check_vma=False,
    )
```
